128 devices in a mesh: shard: 16 (over x_lo, z, core), tensor: 4 (over y), section: 2 (over x_hi).
Axes of the slice: x: 4 (x_hi: 2, x_lo: 2; x = x_hi * 2 + x_lo), y: 4, z: 4, core: 2. Of those that a mesh axis runs over, the one named last changes fastest.
Arguments:
- grads: bfloat16 [2, 4, 16, 2048, 1536], P('section', 'tensor', 'shard'), may hold values from -12 to 12
- gain_grads: float32 [2, 64, 2048], P('section', ('shard', 'tensor')), may hold values from -614 to 614
- master: float32 [2, 4, 1536, 2048], P('section', 'tensor', 'shard'), may hold values from -0.12 to 0.12
- moment1: float32 [2, 4, 1536, 2048], P('section', 'tensor', 'shard'), may hold values from -0.6 to 0.6
- moment2: float32 [2, 4, 1536, 2048], P('section', 'tensor', 'shard'), may hold values from 0.005 to 0.5
- average: float32 [2, 4, 2048, 1536], P('section', 'tensor', 'shard'), may hold values from -0.12 to 0.12
- gain_master: float32 [2, 2048], P('section'), may hold values from 0.5 to 1.5
- gain_m: float32 [2, 2048], P('section'), may hold values from -30 to 30
- gain_v: float32 [2, 2048], P('section'), may hold values from 20 to 2000
Outputs:
- new_master: float32 [2, 4, 1536, 2048], P('section', 'tensor', 'shard')
- new_m: float32 [2, 4, 1536, 2048], P('section', 'tensor', 'shard')
- new_v: float32 [2, 4, 1536, 2048], P('section', 'tensor', 'shard')
- weights: bfloat16 [2, 4, 2048, 1536], P('section', 'tensor')
- new_average: float32 [2, 4, 2048, 1536], P('section', 'tensor', 'shard')
- new_gain: float32 [2, 2048], P('section')
- new_gain_m: float32 [2, 2048], P('section')
- new_gain_v: float32 [2, 2048], P('section')
The draws below stay inside these ranges and needn't reach their ends.
All inputs are finite; a program needn't handle non-finite values.
Results may differ from the reference program's by a relative error of at most 0.001.
Values may be sent and summed in bfloat16 or wider, within the bound.
A program may use at most 128 MiB of HBM per device.

```python
import math
import jax
import jax.numpy as jnp
from jax import lax

D = 2048
BW = 1536
STEP = 10
SECTIONS = 2
N_SHARD = 16
N_TENSOR = 4


def draw_grads(key, part):
    keys = jax.random.split(key, 5)
    shape = (SECTIONS, N_TENSOR, N_SHARD, D, BW)
    row_scale = jnp.exp(jax.random.uniform(keys[0], (SECTIONS, N_TENSOR, 1, D, 1), jnp.float32, 0.0, math.log(10.0)))
    col_scale = jnp.exp(jax.random.uniform(keys[1], (SECTIONS, N_TENSOR, 1, 1, BW), jnp.float32, 0.0, math.log(10.0)))
    col_pos = jnp.arange(BW, dtype=jnp.float32) / float(max(BW - 1, 1))
    trend = jnp.exp(0.5 * math.log(3.0) * col_pos).reshape(1, 1, 1, 1, BW)
    block_pos = jnp.arange(SECTIONS * N_TENSOR, dtype=jnp.float32) / float(max(SECTIONS * N_TENSOR - 1, 1))
    block_scale = jnp.exp(0.5 * math.log(3.0) * block_pos).reshape(SECTIONS, N_TENSOR, 1, 1, 1)
    values = jnp.clip(jax.random.normal(keys[4], shape, jnp.float32), -4.0, 4.0)
    return (0.01 * values * row_scale * col_scale * trend * block_scale).astype(jnp.bfloat16)


def draw_gain_grads(key, part):
    keys = jax.random.split(key, 5)
    count = N_SHARD * N_TENSOR
    shape = (SECTIONS, count, D)
    feature_scale = jnp.exp(jax.random.uniform(keys[0], (SECTIONS, 1, D), jnp.float32, 0.0, math.log(10.0)))
    pairing = jax.random.permutation(keys[1], count).astype(jnp.int32)
    block_of = jnp.arange(D, dtype=jnp.int32) // (D // count)
    spiked = (block_of[None, :] == pairing[:, None]).astype(jnp.float32)
    boost = (1.0 + 3.0 * spiked)[None]
    width_scale = math.sqrt(float(BW))
    values = 0.0937 * width_scale * jnp.clip(jax.random.normal(keys[4], shape, jnp.float32), -4.0, 4.0) * boost
    return (values * feature_scale).astype(jnp.float32)


def levels(own_key, extent, shards, smallest, high):
    loudness = 1.0
    for position, blocks in shards:
        steps = jax.random.uniform(jax.random.fold_in(jax.random.fold_in(own_key, 6), position), (blocks,), jnp.float32, smallest / len(shards), high / len(shards))
        loudness = loudness * jnp.repeat(jnp.exp(steps), extent[position] // blocks).reshape((-1,) + (1,) * (len(extent) - 1 - position))
    return loudness


def scatter_about(stream_key, extent, spread, most, cuts=(), kind=jnp.bfloat16):
    factor_of = levels(stream_key, extent, cuts, -0.22, 0.18) if cuts else 1.0
    entries = jax.random.normal(stream_key, extent, jnp.float32) * spread * factor_of
    return jnp.minimum(jnp.maximum(entries, -most), most).astype(kind)


def setup_inputs(seed: int = 0) -> dict:
    seeds = jax.random.split(jax.random.key(seed), 10)
    return {
        "grads": draw_grads(jax.random.fold_in(seeds[9], 71), 0),
        "gain_grads": draw_gain_grads(jax.random.fold_in(seeds[9], 71), 0),
        "master": scatter_about(seeds[2], (SECTIONS, N_TENSOR, BW, D), 0.02, 0.12, ((0, 2), (1, 4), (2, 16)), jnp.float32),
        "moment1": scatter_about(seeds[3], (SECTIONS, N_TENSOR, BW, D), 0.1, 0.6, ((0, 2), (1, 4), (2, 16)), jnp.float32),
        "moment2": jnp.clip(jnp.exp(math.log(0.5) - 4.6051702 * jax.random.uniform(seeds[4], (SECTIONS, N_TENSOR, BW, D), jnp.float32) ** levels(seeds[4], (SECTIONS, N_TENSOR, BW, D), ((0, 2), (1, 4), (2, 16)), -0.2, 0.2)), 0.005, 0.5),
        "average": scatter_about(seeds[5], (SECTIONS, N_TENSOR, D, BW), 0.02, 0.12, ((0, 2), (1, 4), (2, 16)), jnp.float32),
        "gain_master": jnp.clip(1.0 + 0.1 * jax.random.normal(seeds[6], (SECTIONS, D), jnp.float32), 0.5, 1.5),
        "gain_m": scatter_about(seeds[7], (SECTIONS, D), 6.0, 30.0, ((0, 2),), jnp.float32),
        "gain_v": jnp.clip(jnp.exp(math.log(2000.0) - 4.6051702 * jax.random.uniform(seeds[8], (SECTIONS, D), jnp.float32) ** levels(seeds[8], (SECTIONS, D), ((0, 2),), -0.2, 0.2)), 20.0, 2000.0),
    }


beta_one = 0.9
beta_two = 0.95
learn_rate = 0.01
decay_rate = 0.1
small_eps = 1e-08
average_decay = 0.9

def adamw_update(weight, first, second, grad):
    first_new = beta_one * first + (1.0 - beta_one) * grad
    second_new = beta_two * second + (1.0 - beta_two) * grad * grad
    first_hat = first_new / (1.0 - beta_one ** STEP)
    second_hat = second_new / (1.0 - beta_two ** STEP)
    weight_new = weight - learn_rate * (first_hat / (jnp.sqrt(second_hat) + small_eps) + decay_rate * weight)
    return (weight_new, first_new, second_new)

def reference(grads, gain_grads, master, moment1, moment2, average, gain_master, gain_m, gain_v):

    def accumulate(index, accum):
        return accum + lax.dynamic_index_in_dim(grads, index, 2, keepdims=False).astype(jnp.float32)
    summed = lax.fori_loop(0, N_SHARD, accumulate, jnp.zeros((SECTIONS, N_TENSOR, D, BW), jnp.float32))
    total = jnp.swapaxes(summed, 2, 3)
    gain_total = lax.optimization_barrier(jnp.sum(gain_grads, axis=1))
    squares = jnp.sum(total * total) + jnp.sum(gain_total * gain_total)
    number = float(SECTIONS * N_TENSOR * D * BW + SECTIONS * D)
    rms_value = jnp.sqrt(squares / number + 1e-06)
    clip = jnp.minimum(1.0, 1.0 / rms_value)
    new_master, new_m, new_v = adamw_update(master, moment1, moment2, clip * total)
    new_gain, new_gain_m, new_gain_v = adamw_update(gain_master, gain_m, gain_v, clip * gain_total)
    rows_master = jnp.swapaxes(new_master, 2, 3)
    weights = rows_master.astype(jnp.bfloat16)
    new_average = average_decay * average + (1.0 - average_decay) * rows_master
    return (new_master, new_m, new_v, weights, new_average, new_gain, new_gain_m, new_gain_v)
```

```python
import functools

import jax
import jax.numpy as jnp
from jax import lax
from jax.experimental import pallas as pl
from jax.experimental.pallas import tpu as pltpu
from jax.sharding import PartitionSpec as P

STEP = 10

beta_one = 0.9
beta_two = 0.95
learn_rate = 0.01
decay_rate = 0.1
small_eps = 1e-08
average_decay = 0.9

MESH = pl.DeviceIdType.MESH
F32 = jnp.float32
BF16 = jnp.bfloat16
NX, NZ, NC = 2, 4, 2


def adamw_update(weight, first, second, grad):
    first_new = beta_one * first + (1.0 - beta_one) * grad
    second_new = beta_two * second + (1.0 - beta_two) * grad * grad
    first_hat = first_new / (1.0 - beta_one**STEP)
    second_hat = second_new / (1.0 - beta_two**STEP)
    weight_new = weight - learn_rate * (
        first_hat / (jnp.sqrt(second_hat) + small_eps) + decay_rate * weight
    )
    return (weight_new, first_new, second_new)


def kernel(dims, grads, gain_in, master, mom1, mom2, average, gmaster, gmom1, gmom2,
           o_master, o_m, o_v, o_w, o_avg, o_g, o_gm, o_gv,
           raw, acc, buf1, buf2, buf3, bufb1, bufb2, bufb3, state, wts, low, lowr, avg_in,
           n1, n2, g1, g2, lsem, ssem, rsem, lsend, gsem):
    D, BW, NS, NT = dims
    H = D // 2
    CH = BW // 16
    GR = 2 * CH
    PR = 2 * GR
    XR = NZ * GR
    TL = min(128, H)
    RA = 112 * GR // 192
    RB = GR - RA
    RH = RB // 2
    BH = (48 * RB) // 80
    LR = D // 16

    s = lax.axis_index("shard")
    t = lax.axis_index("tensor")
    sec = lax.axis_index("section")
    x = s // (NZ * NC)
    z = lax.rem(s // NC, NZ)
    c = lax.rem(s, NC)
    xo, co = 1 - x, 1 - c
    p = z // 2

    def shard_of(xx, zz, cc):
        return (xx * NZ + zz) * NC + cc

    zp, zm, zo = lax.rem(z + 1, NZ), lax.rem(z + 3, NZ), lax.rem(z + 2, NZ)
    zf = (2 * p) + 1 - (z - 2 * p)
    zof = lax.rem(zf + 2, NZ)
    to_xn = {"shard": shard_of(xo, z, c)}
    to_zp = {"shard": shard_of(x, zp, c)}
    to_zm = {"shard": shard_of(x, zm, c)}
    to_co = {"shard": shard_of(x, z, co)}

    count = [0]
    started = []

    def send(src, dst, dev):
        k = count[0]
        count[0] += 1
        cp = pltpu.make_async_remote_copy(
            src_ref=src, dst_ref=dst, send_sem=ssem.at[k], recv_sem=rsem.at[k],
            device_id=dev, device_id_type=MESH)
        cp.start()
        started.append(cp)
        return cp

    lcount = [0]

    def local(src, dst):
        k = lcount[0]
        lcount[0] += 1
        cp = pltpu.make_async_copy(src, dst, lsem.at[k])
        cp.start()
        return cp

    def G(xx, zz):
        return pl.multiple_of((xx * NZ + zz) * GR, GR)

    def pair_cols(xx, pp):
        return pl.multiple_of(xx * XR + pp * PR, PR)

    half = pl.multiple_of(c * H, H)
    ohalf = pl.multiple_of(co * H, H)

    order = [(xo, 1 - p), (x, 1 - p), (xo, p), (x, p)]

    own = [local(grads.at[pl.ds(half, H), pl.ds(pair_cols(*q), PR)],
                 raw.at[0, :, pl.ds(pair_cols(*q), PR)]) for q in order]
    c_own = pl.multiple_of(c * CH, CH)
    c_oth = pl.multiple_of(co * CH, CH)
    st_own = [local(ref.at[:, pl.ds(half, H)], state.at[i, pl.ds(c_own, CH), :])
              for i, ref in enumerate((master, mom1, mom2))]
    avg_cp = local(average, avg_in)

    barrier = pltpu.get_barrier_semaphore()
    peers = []
    for i in range(1, 16):
        peers.append({"shard": lax.rem(s + i, 16)})
    sides = []
    for dx in range(NX):
        for ds_ in range(NS):
            for dt in range(NT):
                if dx + ds_ + dt:
                    dev = {"shard": shard_of(lax.rem(x + dx, NX), z, c),
                           "tensor": lax.rem(t + dt, NT),
                           "section": lax.rem(sec + ds_, NS)}
                    sides.append((dx, ds_, dt, dev))
                    if ds_ + dt:
                        peers.append(dev)
    for dev in peers:
        pl.semaphore_signal(barrier, inc=1, device_id=dev, device_id_type=MESH)
    pl.semaphore_wait(barrier, len(peers))

    exch = []
    for q in order:
        cols = pl.ds(pair_cols(*q), PR)
        exch.append(send(grads.at[pl.ds(ohalf, H), cols], raw.at[1, :, cols], to_co))

    slot1 = z * NC + c
    gpeers = []
    for dz in range(NZ):
        for dc in range(NC):
            if dz + dc:
                gpeers.append({"shard": shard_of(x, lax.rem(z + dz, NZ), lax.rem(c + dc, NC))})
    g1[slot1] = gain_in[...]
    gain_cp = [send(gain_in, g1.at[slot1], dev) for dev in gpeers]

    st_oth = [send(ref.at[:, pl.ds(ohalf, H)], state.at[i, pl.ds(c_own, CH), :], to_co)
              for i, ref in enumerate((master, mom1, mom2))]

    def produce(q):
        base = pair_cols(*q)

        @pl.loop(0, PR // 128)
        def _(j):
            cols = pl.ds(pl.multiple_of(base + j * 128, 128), 128)
            for rb in range(H // TL):
                rows = slice(rb * TL, (rb + 1) * TL)
                tile = raw[0, rows, cols].astype(F32) + raw[1, rows, cols].astype(F32)
                acc[cols, rows] = tile.T

    def add(dst_row, buf, rows, block=8):
        @pl.loop(0, rows // block)
        def _(i):
            d = pl.ds(pl.multiple_of(dst_row + i * block, 8), block)
            acc[d, :] = acc[d, :] + buf[pl.ds(pl.multiple_of(i * block, 8), block), :]

    def a_of(xx, zz):
        return acc.at[pl.ds(G(xx, zz), RA), :]

    def b_of(xx, zz, lo=0, n=None):
        return acc.at[pl.ds(pl.multiple_of(G(xx, zz) + RA + lo, 8), RB if n is None else n), :]

    own[0].wait()
    exch[0].wait_recv()
    produce(order[0])
    s_a1m = send(a_of(xo, zo), buf1.at[1], to_zm)
    s_b1 = [send(b_of(xo, zo), bufb1.at[0], to_xn),
            send(b_of(xo, zof), bufb1.at[1], to_xn)]
    own[1].wait()
    exch[1].wait_recv()
    produce(order[1])
    s_a1p = send(a_of(x, zo), buf1.at[0], to_zp)
    own[2].wait()
    exch[2].wait_recv()
    produce(order[2])
    s_b1 += [send(b_of(xo, zf), bufb1.at[2], to_xn),
             send(b_of(xo, z), bufb1.at[3], to_xn)]
    own[3].wait()
    exch[3].wait_recv()
    produce(order[3])
    s_np = send(a_of(xo, zp), buf2.at[0], to_zp)
    s_nm = send(a_of(x, zm), buf2.at[1], to_zm)

    for cp in gain_cp:
        cp.wait_recv()
    gsum = g1[0]
    for i in range(1, NZ * NC):
        gsum = gsum + g1[i]
    slot2 = x * NT + t
    gsem[...] = gsum
    g2[slot2] = gsum
    gain_cp2 = []
    for dx, ds_, dt, dev in sides:
        if ds_ == 0:
            gain_cp2.append(send(gsem, g2.at[slot2], dev))

    s_b1[0].wait_recv()
    add(G(x, zo) + RA, bufb1.at[0], RB)
    s_a1m.wait_recv()
    add(G(xo, zm), buf1.at[1], RA)
    s_dm = send(a_of(xo, zm), buf2.at[2], to_zm)
    s_a1p.wait_recv()
    add(G(x, zp), buf1.at[0], RA)
    s_dp = send(a_of(x, zp), buf2.at[3], to_zp)
    s_b2p = send(b_of(x, zo, 0, RH), bufb2.at[0], to_zp)
    s_b2m = send(b_of(x, zo, RH, RH), bufb2.at[1], to_zm)

    s_b1[1].wait_recv()
    add(G(x, zof) + RA, bufb1.at[1], RB)
    s_b1[2].wait_recv()
    add(G(x, zf) + RA, bufb1.at[2], RB)
    s_b3np = send(b_of(x, zp, RH, RH), bufb3.at[0], to_zp)
    s_b3nm = send(b_of(x, zm, 0, RH), bufb3.at[1], to_zm)

    s_np.wait_recv()
    s_dm.wait_recv()

    @pl.loop(0, RA // 8)
    def _(i):
        d = pl.ds(pl.multiple_of(G(xo, z) + i * 8, 8), 8)
        e = pl.ds(pl.multiple_of(i * 8, 8), 8)
        acc[d, :] = acc[d, :] + buf2[0, e, :] + buf2[2, e, :]

    s_a3 = send(a_of(xo, z), buf3, to_xn)
    s_b2p.wait_recv()
    add(G(x, zp) + RA, bufb2.at[0], RH)
    s_b3dp = send(b_of(x, zp, 0, RH), bufb3.at[2], to_zp)
    s_b2m.wait_recv()
    add(G(x, zm) + RA + RH, bufb2.at[1], RH)
    s_b3dm = send(b_of(x, zm, RH, RH), bufb3.at[3], to_zm)

    s_nm.wait_recv()
    s_dp.wait_recv()

    @pl.loop(0, RA // 8)
    def _(i):
        d = pl.ds(pl.multiple_of(G(x, z) + i * 8, 8), 8)
        e = pl.ds(pl.multiple_of(i * 8, 8), 8)
        acc[d, :] = acc[d, :] + buf2[1, e, :] + buf2[3, e, :]

    s_b1[3].wait_recv()
    add(G(x, z) + RA, bufb1.at[3], RB)

    for cp in gain_cp2:
        cp.wait_recv()
    gain_total = g2[0]
    for i in range(1, NX * NT):
        gain_total = gain_total + g2[i]
    for cp in st_own:
        cp.wait()
    for cp in st_oth:
        cp.wait_recv()

    s_b3np.wait_recv()
    s_b3nm.wait_recv()
    s_b3dp.wait_recv()
    s_b3dm.wait_recv()

    zero = jnp.zeros((8, H), F32)

    def b_rows(lo, from_p, from_m, sq):
        def body(i, carry):
            d = pl.ds(pl.multiple_of(G(x, z) + RA + lo + i * 8, 8), 8)
            e = pl.ds(pl.multiple_of(i * 8, 8), 8)
            v = acc[d, :] + bufb3[from_p, e, :] + bufb3[from_m, e, :]
            acc[d, :] = v
            return carry + v * v
        return lax.fori_loop(0, RH // 8, body, sq)

    sq = b_rows(0, 2, 1, zero)
    sq = b_rows(RH, 0, 3, sq)

    s_a3.wait_recv()

    def a_body(i, carry):
        d = pl.ds(pl.multiple_of(G(x, z) + i * 8, 8), 8)
        e = pl.ds(pl.multiple_of(i * 8, 8), 8)
        v = acc[d, :] + buf3[e, :]
        acc[d, :] = v
        return carry + v * v

    sq = lax.fori_loop(0, RA // 8, a_body, sq)

    LN = min(128, H)
    gsq = gain_total * gain_total
    tile = sq[:, 0:LN]
    gtile = gsq[:, 0:LN]
    for i in range(1, H // LN):
        tile = tile + sq[:, i * LN:(i + 1) * LN]
    for i in range(1, D // LN):
        gtile = gtile + gsq[:, i * LN:(i + 1) * LN]
    tile = tile + gtile * (1.0 / (8 * 16 * NT))
    n1[NZ * NC] = tile
    norm_cp = [send(n1.at[NZ * NC], n1.at[slot1], dev) for dev in gpeers]
    n1[slot1] = tile
    for cp in norm_cp:
        cp.wait_recv()
    tile = n1[0]
    for i in range(1, NZ * NC):
        tile = tile + n1[i]
    slot3 = (x * NS + sec) * NT + t
    n_side = NX * NS * NT
    n2[n_side] = tile
    norm_cp2 = [send(n2.at[n_side], n2.at[slot3], dev) for _, _, _, dev in sides]
    n2[slot3] = tile
    for cp in norm_cp2:
        cp.wait_recv()
    tile = n2[0]
    for i in range(1, n_side):
        tile = tile + n2[i]
    squares = jnp.sum(jnp.sum(tile, axis=0, keepdims=True), axis=1, keepdims=True)
    number = float(NS * NT * D * BW + NS * D)
    rms = jnp.sqrt(squares / number + 1e-06)
    clip = jnp.minimum(1.0, 1.0 / rms)

    mine = G(x, z)

    def update(i, carry):
        e = pl.ds(pl.multiple_of(i * 16, 16), 16)
        d = pl.ds(pl.multiple_of(mine + i * 16, 16), 16)
        nw, nm, nv = adamw_update(state[0, e, :], state[1, e, :], state[2, e, :], clip * acc[d, :])
        state[0, e, :] = nw
        state[1, e, :] = nm
        state[2, e, :] = nv
        hi = nw.astype(BF16)
        wts[c, d, :] = hi
        low[e, :] = (nw - hi.astype(F32)).astype(BF16)
        return carry

    lax.fori_loop(0, GR // 16, update, 0)

    def w_at(h, xx, zz, lo, n):
        return wts.at[h, pl.ds(pl.multiple_of(G(xx, zz) + lo, 16), n), :]

    def relay(xx, zz, lo, n, dev):
        ref = w_at(c, xx, zz, lo, n)
        return send(ref, ref, dev)

    x_a = relay(x, z, 0, RA, to_xn)
    p_a1 = relay(x, z, 0, RA, to_zp)
    m_a1 = relay(x, z, 0, RA, to_zm)
    p_b = relay(x, z, RA, RB, to_zp)
    m_b = relay(x, z, RA, RB, to_zm)
    x_b = [relay(x, z, RA, RB, to_xn)]
    chip = [relay(x, z, 0, GR, to_co)]

    base = count[0]
    count[0] += NZ * NX
    low_cp = []
    for dz in range(NZ):
        for dc in range(NC):
            zz, cc = lax.rem(z + dz, NZ), lax.rem(c + dc, NC)
            src = low.at[:, pl.ds(pl.multiple_of((zz * NC + cc) * LR, LR), LR)]
            cp = pltpu.make_async_remote_copy(
                src_ref=src, dst_ref=lowr.at[pl.ds(mine, GR), :],
                send_sem=lsend.at[dz * NC + dc], recv_sem=rsem.at[base + dz * NX + x],
                device_id={"shard": shard_of(c, zz, cc)}, device_id_type=MESH)
            low_cp.append(cp)
            if dz + dc:
                cp.start()
            else:
                @pl.when(c == x)
                def _():
                    pltpu.make_async_copy(src, lowr.at[pl.ds(mine, GR), :], rsem.at[base + x]).start()

                @pl.when(c != x)
                def _():
                    cp.start()

    x_a.wait_recv()
    p_a2 = relay(xo, z, 0, RA, to_zp)
    m_a2 = relay(xo, z, 0, RA, to_zm)
    chip.append(relay(xo, z, 0, RA, to_co))
    p_a1.wait_recv()
    p_f1 = relay(x, zm, 0, RA, to_zp)
    chip.append(relay(x, zm, 0, RA, to_co))
    m_a1.wait_recv()
    chip.append(relay(x, zp, 0, RA, to_co))
    p_b.wait_recv()
    p_fb = relay(x, zm, RA, BH, to_zp)
    x_b.append(relay(x, zm, RA, RB, to_xn))
    chip.append(relay(x, zm, RA, RB, to_co))
    m_b.wait_recv()
    m_fb = relay(x, zp, RA + BH, RB - BH, to_zm)
    x_b.append(relay(x, zp, RA, RB, to_xn))
    chip.append(relay(x, zp, RA, RB, to_co))
    m_a2.wait_recv()
    m_f1 = relay(xo, zp, 0, RA, to_zm)
    chip.append(relay(xo, zp, 0, RA, to_co))
    p_a2.wait_recv()
    chip.append(relay(xo, zm, 0, RA, to_co))
    p_fb.wait_recv()
    m_fb.wait_recv()
    x_b.append(relay(x, zo, RA, RB, to_xn))
    chip.append(relay(x, zo, RA, RB, to_co))

    outs = (o_master, o_m, o_v)
    out_own = [local(state.at[i, pl.ds(c_own, CH), :], ref.at[:, pl.ds(half, H)])
               for i, ref in enumerate(outs)]
    out_oth = [send(state.at[i, pl.ds(c_oth, CH), :], ref.at[:, pl.ds(half, H)], to_co)
               for i, ref in enumerate(outs)]
    new_g, new_gm, new_gv = adamw_update(gmaster[...], gmom1[...], gmom2[...], clip * gain_total)
    o_g[...] = new_g
    o_gm[...] = new_gm
    o_gv[...] = new_gv

    x_b[0].wait_recv()
    chip.append(relay(xo, z, RA, RB, to_co))
    p_f1.wait_recv()
    chip.append(relay(x, zo, 0, RA, to_co))

    def emit(h, q):
        first = pair_cols(*q)

        @pl.loop(0, PR // 128)
        def _(j):
            cols = pl.ds(pl.multiple_of(first + j * 128, 128), 128)
            for rb in range(H // TL):
                o_w[pl.ds(pl.multiple_of(h * H + rb * TL, TL), TL), cols] = wts[h, cols, rb * TL:(rb + 1) * TL].T

    emit(c, (x, p))
    m_f1.wait_recv()
    chip.append(relay(xo, zo, 0, RA, to_co))
    emit(c, (x, 1 - p))
    x_b[1].wait_recv()
    chip.append(relay(xo, zm, RA, RB, to_co))
    x_b[2].wait_recv()
    chip.append(relay(xo, zp, RA, RB, to_co))
    x_b[3].wait_recv()
    chip.append(relay(xo, zo, RA, RB, to_co))
    emit(c, (xo, p))
    emit(c, (xo, 1 - p))
    for cp in chip:
        cp.wait_recv()
    for q in order:
        emit(co, q)
    for i in range(NZ * NX):
        pltpu.make_async_copy(lowr.at[pl.ds(0, GR), :], lowr.at[pl.ds(0, GR), :], rsem.at[base + i]).wait()
    avg_cp.wait()
    lanes = pl.ds(pl.multiple_of((z * NC + c) * LR, LR), LR)

    @pl.loop(0, BW // 128)
    def _(j):
        cols = pl.ds(pl.multiple_of(j * 128, 128), 128)
        nw = wts[x, cols, lanes].astype(F32) + lowr[cols, :].astype(F32)
        o_avg[:, cols] = average_decay * avg_in[:, cols] + (1.0 - average_decay) * nw.T

    for cp in out_own:
        cp.wait()
    for cp in out_oth:
        cp.wait_recv()
    for cp in started:
        cp.wait_send()
    for i, cp in enumerate(low_cp):
        if i:
            cp.wait_send()
        else:
            @pl.when(c != x)
            def _():
                cp.wait_send()


def local(dims, grads, gain_grads, master, moment1, moment2, average, gain_master, gain_m, gain_v):
    D, BW, NS, NT = dims
    H, CH = D // 2, BW // 16
    GR = 2 * CH
    RA = 112 * GR // 192
    RB = GR - RA
    LN = min(128, H)
    vm, sem = pltpu.VMEM, pltpu.SemaphoreType
    hbm = pl.BlockSpec(memory_space=pltpu.HBM)
    vmem = pl.BlockSpec(memory_space=pltpu.VMEM)
    shape = lambda sh, dt=F32: jax.ShapeDtypeStruct(sh, dt)
    outs = pl.pallas_call(
        functools.partial(kernel, dims),
        out_shape=(shape((CH, D)), shape((CH, D)), shape((CH, D)), shape((D, BW), BF16),
                   shape((D // 16, BW)), shape((1, D)), shape((1, D)), shape((1, D))),
        in_specs=[hbm, vmem, hbm, hbm, hbm, hbm, vmem, vmem, vmem],
        out_specs=[vmem] * 8,
        scratch_shapes=[
            vm((2, H, BW), BF16),
            vm((BW, H), F32),
            vm((2, RA, H), F32),
            vm((4, RA, H), F32),
            vm((RA, H), F32),
            vm((4, RB, H), F32),
            vm((2, RB // 2, H), F32),
            vm((4, RB // 2, H), F32),
            vm((3, GR, H), F32),
            vm((2, BW, H), BF16),
            vm((GR, H), BF16),
            vm((BW, D // 16), BF16),
            vm((D // 16, BW), F32),
            vm((9, 8, LN), F32),
            vm((NX * NS * NT + 1, 8, LN), F32),
            vm((8, 1, D), F32),
            vm((NX * NT, 1, D), F32),
            sem.DMA((16,)),
            sem.DMA((120,)),
            sem.DMA((120,)),
            sem.DMA((8,)),
            vm((1, D), F32),
        ],
        compiler_params=pltpu.CompilerParams(
            collective_id=0, has_side_effects=True, vmem_limit_bytes=48 * 2**20),
        name="adamw_step",
    )(grads[0, 0, 0], gain_grads[0], master[0, 0], moment1[0, 0], moment2[0, 0], average[0, 0],
      gain_master, gain_m, gain_v)
    new_master, new_m, new_v, weights, new_average, g, gm, gv = outs
    return (new_master[None, None], new_m[None, None], new_v[None, None], weights[None, None],
            new_average[None, None], g, gm, gv)


def solution(mesh):
    whole = P("section", "tensor", "shard", None)
    gains = P("section", None)

    def step(grads, *rest):
        dims = (grads.shape[3], grads.shape[4], mesh.shape["section"], mesh.shape["tensor"])
        return jax.shard_map(
            functools.partial(local, dims),
            mesh=mesh,
            in_specs=(P("section", "tensor", "shard", None, None), P("section", ("shard", "tensor"), None),
                      whole, whole, whole, whole, gains, gains, gains),
            out_specs=(whole, whole, whole, P("section", "tensor", None, None), whole, gains, gains, gains),
            check_vma=False,
        )(grads, *rest)

    return step
```

```python
import functools

import jax
import jax.numpy as jnp
from jax import lax
from jax.experimental import pallas as pl
from jax.experimental.pallas import tpu as pltpu
from jax.sharding import PartitionSpec as P

STEP = 10

beta_one = 0.9
beta_two = 0.95
learn_rate = 0.01
decay_rate = 0.1
small_eps = 1e-08
average_decay = 0.9

MESH = pl.DeviceIdType.MESH
F32 = jnp.float32
BF16 = jnp.bfloat16
NX, NZ, NC = 2, 4, 2


def adamw_update(weight, first, second, grad):
    first_new = beta_one * first + (1.0 - beta_one) * grad
    second_new = beta_two * second + (1.0 - beta_two) * grad * grad
    first_hat = first_new / (1.0 - beta_one**STEP)
    second_hat = second_new / (1.0 - beta_two**STEP)
    weight_new = weight - learn_rate * (
        first_hat / (jnp.sqrt(second_hat) + small_eps) + decay_rate * weight
    )
    return (weight_new, first_new, second_new)


def kernel(dims, grads, gain_in, master, mom1, mom2, average, gmaster, gmom1, gmom2,
           o_master, o_m, o_v, o_w, o_avg, o_g, o_gm, o_gv,
           raw, acc, buf1, buf2, buf3, bufb1, bufb2, bufb3, state, wts, low, lowr, avg_in, gbuf,
           n1, n2, g1, g2, lsem, ssem, rsem, lsend, gsem):
    D, BW, NS, NT = dims
    H = D // 2
    CH = BW // 16
    GR = 2 * CH
    PR = 2 * GR
    XR = NZ * GR
    TL = min(128, H)
    RA = 112 * GR // 192
    RB = GR - RA
    RH = RB // 2
    BH = (48 * RB) // 80
    LR = D // 16

    s = lax.axis_index("shard")
    t = lax.axis_index("tensor")
    sec = lax.axis_index("section")
    x = s // (NZ * NC)
    z = lax.rem(s // NC, NZ)
    c = lax.rem(s, NC)
    xo, co = 1 - x, 1 - c
    p = z // 2

    def shard_of(xx, zz, cc):
        return (xx * NZ + zz) * NC + cc

    zp, zm, zo = lax.rem(z + 1, NZ), lax.rem(z + 3, NZ), lax.rem(z + 2, NZ)
    zf = (2 * p) + 1 - (z - 2 * p)
    zof = lax.rem(zf + 2, NZ)
    to_xn = {"shard": shard_of(xo, z, c)}
    to_zp = {"shard": shard_of(x, zp, c)}
    to_zm = {"shard": shard_of(x, zm, c)}
    to_co = {"shard": shard_of(x, z, co)}

    count = [0]
    started = []

    def send(src, dst, dev):
        k = count[0]
        count[0] += 1
        cp = pltpu.make_async_remote_copy(
            src_ref=src, dst_ref=dst, send_sem=ssem.at[k], recv_sem=rsem.at[k],
            device_id=dev, device_id_type=MESH)
        cp.start()
        started.append(cp)
        return cp

    lcount = [0]

    def local(src, dst):
        k = lcount[0]
        lcount[0] += 1
        cp = pltpu.make_async_copy(src, dst, lsem.at[k])
        cp.start()
        return cp

    def G(xx, zz):
        return pl.multiple_of((xx * NZ + zz) * GR, GR)

    def pair_cols(xx, pp):
        return pl.multiple_of(xx * XR + pp * PR, PR)

    half = pl.multiple_of(c * H, H)
    ohalf = pl.multiple_of(co * H, H)

    order = [(xo, 1 - p), (x, 1 - p), (xo, p), (x, p)]

    own = [local(grads.at[pl.ds(half, H), pl.ds(pair_cols(*q), PR)],
                 raw.at[0, :, pl.ds(pair_cols(*q), PR)]) for q in order]
    c_own = pl.multiple_of(c * CH, CH)
    c_oth = pl.multiple_of(co * CH, CH)
    st_own = [local(ref.at[:, pl.ds(half, H)], state.at[i, pl.ds(c_own, CH), :])
              for i, ref in enumerate((master, mom1, mom2))]
    avg_cp = local(average, avg_in)
    gain_own = [local(ref, gbuf.at[i]) for i, ref in enumerate((gain_in, gmaster, gmom1, gmom2))]

    barrier = pltpu.get_barrier_semaphore()
    peers = []
    for i in range(1, 16):
        peers.append({"shard": lax.rem(s + i, 16)})
    sides = []
    for dx in range(NX):
        for ds_ in range(NS):
            for dt in range(NT):
                if dx + ds_ + dt:
                    dev = {"shard": shard_of(lax.rem(x + dx, NX), z, c),
                           "tensor": lax.rem(t + dt, NT),
                           "section": lax.rem(sec + ds_, NS)}
                    sides.append((dx, ds_, dt, dev))
                    if ds_ + dt:
                        peers.append(dev)
    for dev in peers:
        pl.semaphore_signal(barrier, inc=1, device_id=dev, device_id_type=MESH)
    pl.semaphore_wait(barrier, len(peers))

    exch = []
    for q in order:
        cols = pl.ds(pair_cols(*q), PR)
        exch.append(send(grads.at[pl.ds(ohalf, H), cols], raw.at[1, :, cols], to_co))

    slot1 = z * NC + c
    gpeers = []
    for dz in range(NZ):
        for dc in range(NC):
            if dz + dc:
                gpeers.append({"shard": shard_of(x, lax.rem(z + dz, NZ), lax.rem(c + dc, NC))})
    for cp in gain_own:
        cp.wait()
    g1[slot1] = gbuf[0]
    gain_cp = [send(gbuf.at[0], g1.at[slot1], dev) for dev in gpeers]

    st_oth = [send(ref.at[:, pl.ds(ohalf, H)], state.at[i, pl.ds(c_own, CH), :], to_co)
              for i, ref in enumerate((master, mom1, mom2))]

    def produce(q):
        base = pair_cols(*q)

        @pl.loop(0, PR // 128)
        def _(j):
            cols = pl.ds(pl.multiple_of(base + j * 128, 128), 128)
            for rb in range(H // TL):
                rows = slice(rb * TL, (rb + 1) * TL)
                tile = raw[0, rows, cols].astype(F32) + raw[1, rows, cols].astype(F32)
                acc[cols, rows] = tile.T

    def add(dst_row, buf, rows, block=8):
        @pl.loop(0, rows // block)
        def _(i):
            d = pl.ds(pl.multiple_of(dst_row + i * block, 8), block)
            acc[d, :] = acc[d, :] + buf[pl.ds(pl.multiple_of(i * block, 8), block), :]

    def a_of(xx, zz):
        return acc.at[pl.ds(G(xx, zz), RA), :]

    def b_of(xx, zz, lo=0, n=None):
        return acc.at[pl.ds(pl.multiple_of(G(xx, zz) + RA + lo, 8), RB if n is None else n), :]

    own[0].wait()
    exch[0].wait_recv()
    produce(order[0])
    s_a1m = send(a_of(xo, zo), buf1.at[1], to_zm)
    s_b1 = [send(b_of(xo, zo), bufb1.at[0], to_xn),
            send(b_of(xo, zof), bufb1.at[1], to_xn)]
    own[1].wait()
    exch[1].wait_recv()
    produce(order[1])
    s_a1p = send(a_of(x, zo), buf1.at[0], to_zp)
    own[2].wait()
    exch[2].wait_recv()
    produce(order[2])
    s_b1 += [send(b_of(xo, zf), bufb1.at[2], to_xn),
             send(b_of(xo, z), bufb1.at[3], to_xn)]
    own[3].wait()
    exch[3].wait_recv()
    produce(order[3])
    s_np = send(a_of(xo, zp), buf2.at[0], to_zp)
    s_nm = send(a_of(x, zm), buf2.at[1], to_zm)

    for cp in gain_cp:
        cp.wait_recv()
    gsum = g1[0]
    for i in range(1, NZ * NC):
        gsum = gsum + g1[i]
    slot2 = x * NT + t
    gsem[...] = gsum
    g2[slot2] = gsum
    gain_cp2 = []
    for dx, ds_, dt, dev in sides:
        if ds_ == 0:
            gain_cp2.append(send(gsem, g2.at[slot2], dev))

    s_b1[0].wait_recv()
    add(G(x, zo) + RA, bufb1.at[0], RB)
    s_a1m.wait_recv()
    add(G(xo, zm), buf1.at[1], RA)
    s_dm = send(a_of(xo, zm), buf2.at[2], to_zm)
    s_a1p.wait_recv()
    add(G(x, zp), buf1.at[0], RA)
    s_dp = send(a_of(x, zp), buf2.at[3], to_zp)
    s_b2p = send(b_of(x, zo, 0, RH), bufb2.at[0], to_zp)
    s_b2m = send(b_of(x, zo, RH, RH), bufb2.at[1], to_zm)

    s_b1[1].wait_recv()
    add(G(x, zof) + RA, bufb1.at[1], RB)
    s_b1[2].wait_recv()
    add(G(x, zf) + RA, bufb1.at[2], RB)
    s_b3np = send(b_of(x, zp, RH, RH), bufb3.at[0], to_zp)
    s_b3nm = send(b_of(x, zm, 0, RH), bufb3.at[1], to_zm)

    s_np.wait_recv()
    s_dm.wait_recv()

    @pl.loop(0, RA // 8)
    def _(i):
        d = pl.ds(pl.multiple_of(G(xo, z) + i * 8, 8), 8)
        e = pl.ds(pl.multiple_of(i * 8, 8), 8)
        acc[d, :] = acc[d, :] + buf2[0, e, :] + buf2[2, e, :]

    s_a3 = send(a_of(xo, z), buf3, to_xn)
    s_b2p.wait_recv()
    add(G(x, zp) + RA, bufb2.at[0], RH)
    s_b3dp = send(b_of(x, zp, 0, RH), bufb3.at[2], to_zp)
    s_b2m.wait_recv()
    add(G(x, zm) + RA + RH, bufb2.at[1], RH)
    s_b3dm = send(b_of(x, zm, RH, RH), bufb3.at[3], to_zm)

    s_nm.wait_recv()
    s_dp.wait_recv()

    @pl.loop(0, RA // 8)
    def _(i):
        d = pl.ds(pl.multiple_of(G(x, z) + i * 8, 8), 8)
        e = pl.ds(pl.multiple_of(i * 8, 8), 8)
        acc[d, :] = acc[d, :] + buf2[1, e, :] + buf2[3, e, :]

    s_b1[3].wait_recv()
    add(G(x, z) + RA, bufb1.at[3], RB)

    for cp in gain_cp2:
        cp.wait_recv()
    gain_total = g2[0]
    for i in range(1, NX * NT):
        gain_total = gain_total + g2[i]
    for cp in st_own:
        cp.wait()
    for cp in st_oth:
        cp.wait_recv()

    s_b3np.wait_recv()
    s_b3nm.wait_recv()
    s_b3dp.wait_recv()
    s_b3dm.wait_recv()

    zero = jnp.zeros((8, H), F32)

    def b_rows(lo, from_p, from_m, sq):
        def body(i, carry):
            d = pl.ds(pl.multiple_of(G(x, z) + RA + lo + i * 8, 8), 8)
            e = pl.ds(pl.multiple_of(i * 8, 8), 8)
            v = acc[d, :] + bufb3[from_p, e, :] + bufb3[from_m, e, :]
            acc[d, :] = v
            return carry + v * v
        return lax.fori_loop(0, RH // 8, body, sq)

    sq = b_rows(0, 2, 1, zero)
    sq = b_rows(RH, 0, 3, sq)

    s_a3.wait_recv()

    def a_body(i, carry):
        d = pl.ds(pl.multiple_of(G(x, z) + i * 8, 8), 8)
        e = pl.ds(pl.multiple_of(i * 8, 8), 8)
        v = acc[d, :] + buf3[e, :]
        acc[d, :] = v
        return carry + v * v

    sq = lax.fori_loop(0, RA // 8, a_body, sq)

    LN = min(128, H)
    gsq = gain_total * gain_total
    tile = sq[:, 0:LN]
    gtile = gsq[:, 0:LN]
    for i in range(1, H // LN):
        tile = tile + sq[:, i * LN:(i + 1) * LN]
    for i in range(1, D // LN):
        gtile = gtile + gsq[:, i * LN:(i + 1) * LN]
    tile = tile + gtile * (1.0 / (8 * 16 * NT))
    n1[NZ * NC] = tile
    norm_cp = [send(n1.at[NZ * NC], n1.at[slot1], dev) for dev in gpeers]
    n1[slot1] = tile
    for cp in norm_cp:
        cp.wait_recv()
    tile = n1[0]
    for i in range(1, NZ * NC):
        tile = tile + n1[i]
    slot3 = (x * NS + sec) * NT + t
    n_side = NX * NS * NT
    n2[n_side] = tile
    norm_cp2 = [send(n2.at[n_side], n2.at[slot3], dev) for _, _, _, dev in sides]
    n2[slot3] = tile
    for cp in norm_cp2:
        cp.wait_recv()
    tile = n2[0]
    for i in range(1, n_side):
        tile = tile + n2[i]
    squares = jnp.sum(jnp.sum(tile, axis=0, keepdims=True), axis=1, keepdims=True)
    number = float(NS * NT * D * BW + NS * D)
    rms = jnp.sqrt(squares / number + 1e-06)
    clip = jnp.minimum(1.0, 1.0 / rms)

    mine = G(x, z)

    def update(i, carry):
        e = pl.ds(pl.multiple_of(i * 16, 16), 16)
        d = pl.ds(pl.multiple_of(mine + i * 16, 16), 16)
        nw, nm, nv = adamw_update(state[0, e, :], state[1, e, :], state[2, e, :], clip * acc[d, :])
        state[0, e, :] = nw
        state[1, e, :] = nm
        state[2, e, :] = nv
        hi = nw.astype(BF16)
        wts[c, d, :] = hi
        low[e, :] = (nw - hi.astype(F32)).astype(BF16)
        return carry

    def w_at(h, xx, zz, lo, n):
        return wts.at[h, pl.ds(pl.multiple_of(G(xx, zz) + lo, 16), n), :]

    def relay(xx, zz, lo, n, dev):
        ref = w_at(c, xx, zz, lo, n)
        return send(ref, ref, dev)

    lax.fori_loop(0, RA // 16, update, 0)
    x_a = relay(x, z, 0, RA, to_xn)
    p_a1 = relay(x, z, 0, RA, to_zp)
    m_a1 = relay(x, z, 0, RA, to_zm)
    lax.fori_loop(RA // 16, GR // 16, update, 0)
    p_b = relay(x, z, RA, RB, to_zp)
    m_b = relay(x, z, RA, RB, to_zm)
    x_b = [relay(x, z, RA, RB, to_xn)]

    def on_chip(xx, zz, lo, n):
        return relay(xx, zz, lo, n, to_co)

    k_own = on_chip(x, z, 0, GR)

    def emit(h, q):
        first = pair_cols(*q)

        @pl.loop(0, PR // 128)
        def _(j):
            cols = pl.ds(pl.multiple_of(first + j * 128, 128), 128)
            for rb in range(H // TL):
                o_w[pl.ds(pl.multiple_of(h * H + rb * TL, TL), TL), cols] = wts[h, cols, rb * TL:(rb + 1) * TL].T

    outs = (o_master, o_m, o_v)
    out_own = [local(state.at[i, pl.ds(c_own, CH), :], ref.at[:, pl.ds(half, H)])
               for i, ref in enumerate(outs)]
    new_g, new_gm, new_gv = adamw_update(gbuf[1], gbuf[2], gbuf[3], clip * gain_total)
    o_g[...] = new_g
    o_gm[...] = new_gm
    o_gv[...] = new_gv

    x_a.wait_recv()
    p_a2 = relay(xo, z, 0, RA, to_zp)
    m_a2 = relay(xo, z, 0, RA, to_zm)
    k_xa = on_chip(xo, z, 0, RA)
    p_a1.wait_recv()
    k_ma = on_chip(x, zm, 0, RA)
    m_a1.wait_recv()
    k_pa = on_chip(x, zp, 0, RA)
    p_b.wait_recv()
    x_b.append(relay(x, zm, RA, RB, to_xn))
    p_fb = relay(x, zm, RA, BH, to_zp)
    k_mb = on_chip(x, zm, RA, RB)
    m_b.wait_recv()
    x_b.append(relay(x, zp, RA, RB, to_xn))
    m_fb = relay(x, zp, RA + BH, RB - BH, to_zm)
    k_pb = on_chip(x, zp, RA, RB)
    p_f1 = relay(x, zm, 0, RA, to_zp)
    x_b[0].wait_recv()
    k_xb = on_chip(xo, z, RA, RB)
    emit(c, (x, p))
    m_a2.wait_recv()
    m_f1 = relay(xo, zp, 0, RA, to_zm)
    k_xpa = on_chip(xo, zp, 0, RA)
    p_a2.wait_recv()
    k_xma = on_chip(xo, zm, 0, RA)
    out_oth = [send(state.at[i, pl.ds(c_oth, CH), :], ref.at[:, pl.ds(half, H)], to_co)
               for i, ref in enumerate(outs)]
    for cp in (k_own, k_ma, k_pa, k_mb, k_pb):
        cp.wait_recv()
    emit(co, (x, p))
    p_fb.wait_recv()
    m_fb.wait_recv()
    x_b.append(relay(x, zo, RA, RB, to_xn))
    k_ob = on_chip(x, zo, RA, RB)

    base = count[0]
    count[0] += NZ * NX
    low_cp = []
    for dz in range(NZ):
        for dc in range(NC):
            zz, cc = lax.rem(z + dz, NZ), lax.rem(c + dc, NC)
            src = low.at[:, pl.ds(pl.multiple_of((zz * NC + cc) * LR, LR), LR)]
            cp = pltpu.make_async_remote_copy(
                src_ref=src, dst_ref=lowr.at[pl.ds(mine, GR), :],
                send_sem=lsend.at[dz * NC + dc], recv_sem=rsem.at[base + dz * NX + x],
                device_id={"shard": shard_of(c, zz, cc)}, device_id_type=MESH)
            low_cp.append(cp)
            if dz + dc:
                cp.start()
            else:
                @pl.when(c == x)
                def _():
                    pltpu.make_async_copy(src, lowr.at[pl.ds(mine, GR), :], rsem.at[base + x]).start()

                @pl.when(c != x)
                def _():
                    cp.start()

    x_b[1].wait_recv()
    k_xmb = on_chip(xo, zm, RA, RB)
    x_b[2].wait_recv()
    k_xpb = on_chip(xo, zp, RA, RB)
    emit(c, (xo, p))
    for cp in (k_xa, k_xb, k_xpa, k_xma, k_xmb, k_xpb):
        cp.wait_recv()
    emit(co, (xo, p))
    p_f1.wait_recv()
    k_oa = on_chip(x, zo, 0, RA)
    m_f1.wait_recv()
    k_xoa = on_chip(xo, zo, 0, RA)
    x_b[3].wait_recv()
    k_xob = on_chip(xo, zo, RA, RB)
    emit(c, (x, 1 - p))
    for cp in (k_ob, k_oa):
        cp.wait_recv()
    emit(co, (x, 1 - p))
    emit(c, (xo, 1 - p))
    for cp in (k_xoa, k_xob):
        cp.wait_recv()
    emit(co, (xo, 1 - p))
    for i in range(NZ * NX):
        pltpu.make_async_copy(lowr.at[pl.ds(0, GR), :], lowr.at[pl.ds(0, GR), :], rsem.at[base + i]).wait()
    avg_cp.wait()
    lanes = pl.ds(pl.multiple_of((z * NC + c) * LR, LR), LR)

    @pl.loop(0, BW // 128)
    def _(j):
        cols = pl.ds(pl.multiple_of(j * 128, 128), 128)
        nw = wts[x, cols, lanes].astype(F32) + lowr[cols, :].astype(F32)
        o_avg[:, cols] = average_decay * avg_in[:, cols] + (1.0 - average_decay) * nw.T

    for cp in out_own:
        cp.wait()
    for cp in out_oth:
        cp.wait_recv()
    for cp in started:
        cp.wait_send()
    for i, cp in enumerate(low_cp):
        if i:
            cp.wait_send()
        else:
            @pl.when(c != x)
            def _():
                cp.wait_send()


def store(*refs):
    sems = refs[-1]
    n = (len(refs) - 1) // 2
    copies = []
    for src, dst in zip(refs[:n], refs[n:2 * n]):
        rows = src.shape[0]
        parts = 8 if rows % 128 == 0 and rows > 1024 else 1
        for i in range(parts):
            r = pl.ds(i * (rows // parts), rows // parts)
            copies.append(pltpu.make_async_copy(src.at[r, :], dst.at[r, :], sems.at[len(copies)]))
    for cp in copies:
        cp.start()
    for cp in copies:
        cp.wait()


def local(dims, grads, gain_grads, master, moment1, moment2, average, gain_master, gain_m, gain_v):
    D, BW, NS, NT = dims
    H, CH = D // 2, BW // 16
    GR = 2 * CH
    RA = 112 * GR // 192
    RB = GR - RA
    LN = min(128, H)
    vm, sem = pltpu.VMEM, pltpu.SemaphoreType
    hbm = pl.BlockSpec(memory_space=pltpu.HBM)
    vmem = pl.BlockSpec(memory_space=pltpu.VMEM)
    shape = lambda sh, dt=F32: jax.ShapeDtypeStruct(sh, dt)
    outs = pl.pallas_call(
        functools.partial(kernel, dims),
        out_shape=(shape((CH, D)), shape((CH, D)), shape((CH, D)), shape((D, BW), BF16),
                   shape((D // 16, BW)), shape((1, D)), shape((1, D)), shape((1, D))),
        in_specs=[hbm] * 9,
        out_specs=[vmem] * 8,
        scratch_shapes=[
            vm((2, H, BW), BF16),
            vm((BW, H), F32),
            vm((2, RA, H), F32),
            vm((4, RA, H), F32),
            vm((RA, H), F32),
            vm((4, RB, H), F32),
            vm((2, RB // 2, H), F32),
            vm((4, RB // 2, H), F32),
            vm((3, GR, H), F32),
            vm((2, BW, H), BF16),
            vm((GR, H), BF16),
            vm((BW, D // 16), BF16),
            vm((D // 16, BW), F32),
            vm((4, 1, D), F32),
            vm((9, 8, LN), F32),
            vm((NX * NS * NT + 1, 8, LN), F32),
            vm((8, 1, D), F32),
            vm((NX * NT, 1, D), F32),
            sem.DMA((24,)),
            sem.DMA((120,)),
            sem.DMA((120,)),
            sem.DMA((8,)),
            vm((1, D), F32),
        ],
        compiler_params=pltpu.CompilerParams(
            collective_id=0, has_side_effects=True, vmem_limit_bytes=34 * 2**20),
        name="adamw_step",
    )(*[pltpu.with_memory_space_constraint(a, pltpu.HBM) for a in (
        grads[0, 0, 0], gain_grads[0], master[0, 0], moment1[0, 0], moment2[0, 0], average[0, 0],
        gain_master, gain_m, gain_v)])
    outs = pl.pallas_call(
        store,
        out_shape=[shape(o.shape, o.dtype) for o in outs],
        in_specs=[pl.BlockSpec(memory_space=pl.ANY)] * 8,
        out_specs=[pl.BlockSpec(memory_space=pl.ANY)] * 8,
        scratch_shapes=[sem.DMA((16,))],
        compiler_params=pltpu.CompilerParams(vmem_limit_bytes=2**20),
        name="store",
    )(*outs)
    new_master, new_m, new_v, weights, new_average, g, gm, gv = outs
    return (new_master[None, None], new_m[None, None], new_v[None, None], weights[None, None],
            new_average[None, None], g, gm, gv)


def solution(mesh):
    whole = P("section", "tensor", "shard", None)
    gains = P("section", None)

    def step(grads, *rest):
        dims = (grads.shape[3], grads.shape[4], mesh.shape["section"], mesh.shape["tensor"])
        return jax.shard_map(
            functools.partial(local, dims),
            mesh=mesh,
            in_specs=(P("section", "tensor", "shard", None, None), P("section", ("shard", "tensor"), None),
                      whole, whole, whole, whole, gains, gains, gains),
            out_specs=(whole, whole, whole, P("section", "tensor", None, None), whole, gains, gains, gains),
            check_vma=False,
        )(grads, *rest)

    return step
```

```python
import functools

import jax
import jax.numpy as jnp
from jax import lax
from jax.experimental import pallas as pl
from jax.experimental.pallas import tpu as pltpu
from jax.sharding import PartitionSpec as P

STEP = 10

beta_one = 0.9
beta_two = 0.95
learn_rate = 0.01
decay_rate = 0.1
small_eps = 1e-08
average_decay = 0.9

MESH = pl.DeviceIdType.MESH
F32 = jnp.float32
BF16 = jnp.bfloat16
NX, NZ, NC = 2, 4, 2


def adamw_update(weight, first, second, grad):
    first_new = beta_one * first + (1.0 - beta_one) * grad
    second_new = beta_two * second + (1.0 - beta_two) * grad * grad
    first_hat = first_new / (1.0 - beta_one**STEP)
    second_hat = second_new / (1.0 - beta_two**STEP)
    weight_new = weight - learn_rate * (
        first_hat / (jnp.sqrt(second_hat) + small_eps) + decay_rate * weight
    )
    return (weight_new, first_new, second_new)


def kernel(dims, grads, gain_in, master, mom1, mom2, average, gmaster, gmom1, gmom2,
           o_master, o_m, o_v, o_w, o_avg, o_g, o_gm, o_gv,
           raw, acc, buf1, buf2, buf3, bufb1, bufb2, bufb3, state, wts, low, lowr, avg_in, gbuf, pre,
           n1, n2, g1, g2, lsem, ssem, rsem, lsend, gsem):
    D, BW, NS, NT = dims
    H = D // 2
    CH = BW // 16
    GR = 2 * CH
    PR = 2 * GR
    XR = NZ * GR
    TL = min(128, H)
    RA = 112 * GR // 192
    RB = GR - RA
    RH = RB // 2
    AH = RA // 2
    BH = (48 * RB) // 80
    LR = D // 16

    s = lax.axis_index("shard")
    t = lax.axis_index("tensor")
    sec = lax.axis_index("section")
    x = s // (NZ * NC)
    z = lax.rem(s // NC, NZ)
    c = lax.rem(s, NC)
    xo, co = 1 - x, 1 - c
    p = z // 2

    def shard_of(xx, zz, cc):
        return (xx * NZ + zz) * NC + cc

    zp, zm, zo = lax.rem(z + 1, NZ), lax.rem(z + 3, NZ), lax.rem(z + 2, NZ)
    zf = (2 * p) + 1 - (z - 2 * p)
    zof = lax.rem(zf + 2, NZ)
    to_xn = {"shard": shard_of(xo, z, c)}
    to_zp = {"shard": shard_of(x, zp, c)}
    to_zm = {"shard": shard_of(x, zm, c)}
    to_co = {"shard": shard_of(x, z, co)}

    count = [0]
    started = []

    def send(src, dst, dev):
        k = count[0]
        count[0] += 1
        cp = pltpu.make_async_remote_copy(
            src_ref=src, dst_ref=dst, send_sem=ssem.at[k], recv_sem=rsem.at[k],
            device_id=dev, device_id_type=MESH)
        cp.start()
        started.append(cp)
        return cp

    lcount = [0]

    def local(src, dst):
        k = lcount[0]
        lcount[0] += 1
        cp = pltpu.make_async_copy(src, dst, lsem.at[k])
        cp.start()
        return cp

    def G(xx, zz):
        return pl.multiple_of((xx * NZ + zz) * GR, GR)

    def pair_cols(xx, pp):
        return pl.multiple_of(xx * XR + pp * PR, PR)

    half = pl.multiple_of(c * H, H)
    ohalf = pl.multiple_of(co * H, H)

    order = [(xo, 1 - p), (x, 1 - p), (xo, p), (x, p)]

    odd = lax.rem(z, 2)
    early = [(0, 0), (0, 1), (1, 0), (1, 1), (0, 2), (1, 2)]

    own = [local(grads.at[pl.ds(half, H), pl.ds(pair_cols(*q), PR)],
                 raw.at[0, :, pl.ds(pair_cols(*q), PR)]) for q in order]
    early_cols = [pl.ds(pl.multiple_of(pair_cols(*order[u]) + (k + odd * (2 - 2 * k)) * 128, 128), 128)
                  for u, k in early]
    ahead = [local(grads.at[pl.ds(ohalf, H), cols], pre.at[i]) for i, cols in enumerate(early_cols)]
    c_own = pl.multiple_of(c * CH, CH)
    c_oth = pl.multiple_of(co * CH, CH)
    st_own = [local(ref.at[:, pl.ds(half, H)], state.at[i, pl.ds(c_own, CH), :])
              for i, ref in enumerate((master, mom1, mom2))]
    avg_cp = local(average, avg_in)
    gain_own = [local(ref, gbuf.at[i]) for i, ref in enumerate((gain_in, gmaster, gmom1, gmom2))]

    barrier = pltpu.get_barrier_semaphore()
    peers = []
    for i in range(1, 16):
        peers.append({"shard": lax.rem(s + i, 16)})
    sides = []
    for dx in range(NX):
        for ds_ in range(NS):
            for dt in range(NT):
                if dx + ds_ + dt:
                    dev = {"shard": shard_of(lax.rem(x + dx, NX), z, c),
                           "tensor": lax.rem(t + dt, NT),
                           "section": lax.rem(sec + ds_, NS)}
                    sides.append((dx, ds_, dt, dev))
                    if ds_ + dt:
                        peers.append(dev)
    for dev in peers:
        pl.semaphore_signal(barrier, inc=1, device_id=dev, device_id_type=MESH)
    pl.semaphore_wait(barrier, len(peers))

    exch = []
    for i, cols in enumerate(early_cols):
        ahead[i].wait()
        exch.append(send(pre.at[i], raw.at[1, :, cols], to_co))
    for q in order[2:]:
        cols = pl.ds(pair_cols(*q), PR)
        exch.append(send(grads.at[pl.ds(ohalf, H), cols], raw.at[1, :, cols], to_co))

    slot1 = z * NC + c
    gpeers = []
    for dz in range(NZ):
        for dc in range(NC):
            if dz + dc:
                gpeers.append({"shard": shard_of(x, lax.rem(z + dz, NZ), lax.rem(c + dc, NC))})
    for cp in gain_own:
        cp.wait()
    g1[slot1] = gbuf[0]
    gain_cp = [send(gbuf.at[0], g1.at[slot1], dev) for dev in gpeers]

    st_oth = [send(ref.at[:, pl.ds(ohalf, H)], state.at[i, pl.ds(c_own, CH), :], to_co)
              for i, ref in enumerate((master, mom1, mom2))]

    def produce_tile(cols):
        for rb in range(H // TL):
            rows = slice(rb * TL, (rb + 1) * TL)
            tile = raw[0, rows, cols].astype(F32) + raw[1, rows, cols].astype(F32)
            acc[cols, rows] = tile.T

    def produce(q):
        base = pair_cols(*q)

        @pl.loop(0, PR // 128)
        def _(j):
            produce_tile(pl.ds(pl.multiple_of(base + j * 128, 128), 128))

    def add(dst_row, buf, rows, block=8):
        @pl.loop(0, rows // block)
        def _(i):
            d = pl.ds(pl.multiple_of(dst_row + i * block, 8), block)
            acc[d, :] = acc[d, :] + buf[pl.ds(pl.multiple_of(i * block, 8), block), :]

    def a_of(xx, zz, lo=0, n=None):
        return acc.at[pl.ds(pl.multiple_of(G(xx, zz) + lo, 8), RA if n is None else n), :]

    def b_of(xx, zz, lo=0, n=None):
        return acc.at[pl.ds(pl.multiple_of(G(xx, zz) + RA + lo, 8), RB if n is None else n), :]

    own[0].wait()
    own[1].wait()
    for i, (u, k) in enumerate(early):
        exch[i].wait_recv()
        produce_tile(early_cols[i])
        if i == 1:
            s_b1 = [send(b_of(xo, zo), bufb1.at[0], to_xn)]
            s_a1p = [send(a_of(xo, zo, AH, AH), buf1.at[0, 0], to_zp)]
            s_a1m = [send(a_of(xo, zo, 0, AH), buf1.at[0, 1], to_zm)]
        elif i == 3:
            s_a1p.append(send(a_of(x, zo, AH, AH), buf1.at[1, 0], to_zp))
            s_a1m.append(send(a_of(x, zo, 0, AH), buf1.at[1, 1], to_zm))
        elif i == 4:
            s_b1.append(send(b_of(xo, zof), bufb1.at[1], to_xn))
    own[2].wait()
    exch[6].wait_recv()
    produce(order[2])
    s_b1 += [send(b_of(xo, zf), bufb1.at[2], to_xn),
             send(b_of(xo, z), bufb1.at[3], to_xn)]
    own[3].wait()
    exch[7].wait_recv()
    produce(order[3])
    s_np = [send(a_of(xo, zp, 0, AH), buf2.at[0, 0], to_zp)]
    s_nm = [send(a_of(xo, zm, AH, AH), buf2.at[0, 1], to_zm)]

    for cp in gain_cp:
        cp.wait_recv()
    gsum = g1[0]
    for i in range(1, NZ * NC):
        gsum = gsum + g1[i]
    slot2 = x * NT + t
    gsem[...] = gsum
    g2[slot2] = gsum
    gain_cp2 = []
    for dx, ds_, dt, dev in sides:
        if ds_ == 0:
            gain_cp2.append(send(gsem, g2.at[slot2], dev))

    s_b1[0].wait_recv()
    add(G(x, zo) + RA, bufb1.at[0], RB)
    s_dp, s_dm = [], []
    for i, xx in enumerate((xo, x)):
        s_a1p[i].wait_recv()
        add(G(xx, zp) + AH, buf1.at[i, 0], AH)
        s_dp.append(send(a_of(xx, zp, AH, AH), buf2.at[i, 2], to_zp))
        s_a1m[i].wait_recv()
        add(G(xx, zm), buf1.at[i, 1], AH)
        s_dm.append(send(a_of(xx, zm, 0, AH), buf2.at[i, 3], to_zm))
        if i == 0:
            s_np.append(send(a_of(x, zp, 0, AH), buf2.at[1, 0], to_zp))
            s_nm.append(send(a_of(x, zm, AH, AH), buf2.at[1, 1], to_zm))
    s_b2p = send(b_of(x, zo, 0, RH), bufb2.at[0], to_zp)
    s_b2m = send(b_of(x, zo, RH, RH), bufb2.at[1], to_zm)

    s_b1[1].wait_recv()
    add(G(x, zof) + RA, bufb1.at[1], RB)
    s_b1[2].wait_recv()
    add(G(x, zf) + RA, bufb1.at[2], RB)
    s_b3np = send(b_of(x, zp, RH, RH), bufb3.at[0], to_zp)
    s_b3nm = send(b_of(x, zm, 0, RH), bufb3.at[1], to_zm)

    def meet(xx, i, lo, plain, summed):
        @pl.loop(0, AH // 8)
        def _(j):
            d = pl.ds(pl.multiple_of(G(xx, z) + lo + j * 8, 8), 8)
            e = pl.ds(pl.multiple_of(j * 8, 8), 8)
            acc[d, :] = acc[d, :] + buf2[i, plain, e, :] + buf2[i, summed, e, :]

    s_np[0].wait_recv()
    s_nm[0].wait_recv()
    s_a3 = []
    s_dm[0].wait_recv()
    meet(xo, 0, 0, 0, 3)
    s_a3.append(send(a_of(xo, z, 0, AH), buf3.at[pl.ds(0, AH), :], to_xn))
    s_dp[0].wait_recv()
    meet(xo, 0, AH, 1, 2)
    s_a3.append(send(a_of(xo, z, AH, AH), buf3.at[pl.ds(AH, AH), :], to_xn))
    s_b2p.wait_recv()
    add(G(x, zp) + RA, bufb2.at[0], RH)
    s_b3dp = send(b_of(x, zp, 0, RH), bufb3.at[2], to_zp)
    s_b2m.wait_recv()
    add(G(x, zm) + RA + RH, bufb2.at[1], RH)
    s_b3dm = send(b_of(x, zm, RH, RH), bufb3.at[3], to_zm)

    for cp in (s_np[1], s_nm[1], s_dm[1], s_dp[1]):
        cp.wait_recv()
    meet(x, 1, 0, 0, 3)
    meet(x, 1, AH, 1, 2)

    s_b1[3].wait_recv()
    add(G(x, z) + RA, bufb1.at[3], RB)

    for cp in gain_cp2:
        cp.wait_recv()
    gain_total = g2[0]
    for i in range(1, NX * NT):
        gain_total = gain_total + g2[i]
    for cp in st_own:
        cp.wait()
    for cp in st_oth:
        cp.wait_recv()

    s_b3np.wait_recv()
    s_b3nm.wait_recv()
    s_b3dp.wait_recv()
    s_b3dm.wait_recv()

    zero = jnp.zeros((8, H), F32)

    def b_rows(lo, from_p, from_m, sq):
        def body(i, carry):
            d = pl.ds(pl.multiple_of(G(x, z) + RA + lo + i * 8, 8), 8)
            e = pl.ds(pl.multiple_of(i * 8, 8), 8)
            v = acc[d, :] + bufb3[from_p, e, :] + bufb3[from_m, e, :]
            acc[d, :] = v
            return carry + v * v
        return lax.fori_loop(0, RH // 8, body, sq)

    sq = b_rows(0, 2, 1, zero)
    sq = b_rows(RH, 0, 3, sq)

    def a_body(i, carry):
        d = pl.ds(pl.multiple_of(G(x, z) + i * 8, 8), 8)
        e = pl.ds(pl.multiple_of(i * 8, 8), 8)
        v = acc[d, :] + buf3[e, :]
        acc[d, :] = v
        return carry + v * v

    for i, cp in enumerate(s_a3):
        cp.wait_recv()
        sq = lax.fori_loop(i * AH // 8, (i + 1) * AH // 8, a_body, sq)

    LN = min(128, H)
    gsq = gain_total * gain_total
    tile = sq[:, 0:LN]
    gtile = gsq[:, 0:LN]
    for i in range(1, H // LN):
        tile = tile + sq[:, i * LN:(i + 1) * LN]
    for i in range(1, D // LN):
        gtile = gtile + gsq[:, i * LN:(i + 1) * LN]
    tile = tile + gtile * (1.0 / (8 * 16 * NT))
    n1[NZ * NC] = tile
    norm_cp = [send(n1.at[NZ * NC], n1.at[slot1], dev) for dev in gpeers]
    n1[slot1] = tile
    for cp in norm_cp:
        cp.wait_recv()
    tile = n1[0]
    for i in range(1, NZ * NC):
        tile = tile + n1[i]
    slot3 = (x * NS + sec) * NT + t
    n_side = NX * NS * NT
    n2[n_side] = tile
    norm_cp2 = [send(n2.at[n_side], n2.at[slot3], dev) for _, _, _, dev in sides]
    n2[slot3] = tile
    for cp in norm_cp2:
        cp.wait_recv()
    tile = n2[0]
    for i in range(1, n_side):
        tile = tile + n2[i]
    squares = jnp.sum(jnp.sum(tile, axis=0, keepdims=True), axis=1, keepdims=True)
    number = float(NS * NT * D * BW + NS * D)
    rms = jnp.sqrt(squares / number + 1e-06)
    clip = jnp.minimum(1.0, 1.0 / rms)

    mine = G(x, z)

    def update(i, carry):
        e = pl.ds(pl.multiple_of(i * 16, 16), 16)
        d = pl.ds(pl.multiple_of(mine + i * 16, 16), 16)
        nw, nm, nv = adamw_update(state[0, e, :], state[1, e, :], state[2, e, :], clip * acc[d, :])
        state[0, e, :] = nw
        state[1, e, :] = nm
        state[2, e, :] = nv
        hi = nw.astype(BF16)
        wts[c, d, :] = hi
        low[e, :] = (nw - hi.astype(F32)).astype(BF16)
        return carry

    def w_at(h, xx, zz, lo, n):
        return wts.at[h, pl.ds(pl.multiple_of(G(xx, zz) + lo, 16), n), :]

    def relay(xx, zz, lo, n, dev):
        ref = w_at(c, xx, zz, lo, n)
        return send(ref, ref, dev)

    x_a, p_a1, m_a1 = [], [], []
    for lo, n in ((0, 48), (48, RA - 48)):
        lax.fori_loop(lo // 16, (lo + n) // 16, update, 0)
        x_a.append(relay(x, z, lo, n, to_xn))
        p_a1.append(relay(x, z, lo, n, to_zp))
        m_a1.append(relay(x, z, lo, n, to_zm))
    lax.fori_loop(RA // 16, GR // 16, update, 0)
    p_b = relay(x, z, RA, RB, to_zp)
    m_b = relay(x, z, RA, RB, to_zm)
    x_b = [relay(x, z, RA, RB, to_xn)]

    def on_chip(xx, zz, lo, n):
        return relay(xx, zz, lo, n, to_co)

    k_own = on_chip(x, z, 0, GR)

    def emit(h, q):
        first = pair_cols(*q)

        @pl.loop(0, PR // 128)
        def _(j):
            cols = pl.ds(pl.multiple_of(first + j * 128, 128), 128)
            for rb in range(H // TL):
                o_w[pl.ds(pl.multiple_of(h * H + rb * TL, TL), TL), cols] = wts[h, cols, rb * TL:(rb + 1) * TL].T

    outs = (o_master, o_m, o_v)
    out_own = [local(state.at[i, pl.ds(c_own, CH), :], ref.at[:, pl.ds(half, H)])
               for i, ref in enumerate(outs)]
    new_g, new_gm, new_gv = adamw_update(gbuf[1], gbuf[2], gbuf[3], clip * gain_total)
    o_g[...] = new_g
    o_gm[...] = new_gm
    o_gv[...] = new_gv

    for cp in x_a:
        cp.wait_recv()
    p_a2 = relay(xo, z, 0, RA, to_zp)
    m_a2 = relay(xo, z, 0, RA, to_zm)
    k_xa = on_chip(xo, z, 0, RA)
    for cp in p_a1:
        cp.wait_recv()
    k_ma = on_chip(x, zm, 0, RA)
    for cp in m_a1:
        cp.wait_recv()
    k_pa = on_chip(x, zp, 0, RA)
    p_b.wait_recv()
    x_b.append(relay(x, zm, RA, RB, to_xn))
    p_fb = relay(x, zm, RA, BH, to_zp)
    k_mb = on_chip(x, zm, RA, RB)
    m_b.wait_recv()
    x_b.append(relay(x, zp, RA, RB, to_xn))
    m_fb = relay(x, zp, RA + BH, RB - BH, to_zm)
    k_pb = on_chip(x, zp, RA, RB)
    p_f1 = relay(x, zm, 0, RA, to_zp)
    x_b[0].wait_recv()
    k_xb = on_chip(xo, z, RA, RB)
    emit(c, (x, p))
    m_a2.wait_recv()
    m_f1 = relay(xo, zp, 0, RA, to_zm)
    k_xpa = on_chip(xo, zp, 0, RA)
    p_a2.wait_recv()
    k_xma = on_chip(xo, zm, 0, RA)
    out_oth = [send(state.at[i, pl.ds(c_oth, CH), :], ref.at[:, pl.ds(half, H)], to_co)
               for i, ref in enumerate(outs)]
    for cp in (k_own, k_ma, k_pa, k_mb, k_pb):
        cp.wait_recv()
    emit(co, (x, p))
    p_fb.wait_recv()
    m_fb.wait_recv()
    x_b.append(relay(x, zo, RA, RB, to_xn))
    k_ob = on_chip(x, zo, RA, RB)

    base = count[0]
    count[0] += NZ * NX
    low_cp = []
    for dz in (0, 1, 3, 2):
        for dc in range(NC):
            zz, cc = lax.rem(z + dz, NZ), lax.rem(c + dc, NC)
            src = low.at[:, pl.ds(pl.multiple_of((zz * NC + cc) * LR, LR), LR)]
            cp = pltpu.make_async_remote_copy(
                src_ref=src, dst_ref=lowr.at[pl.ds(mine, GR), :],
                send_sem=lsend.at[dz * NC + dc], recv_sem=rsem.at[base + dz * NX + x],
                device_id={"shard": shard_of(c, zz, cc)}, device_id_type=MESH)
            low_cp.append(cp)
            if dz + dc:
                cp.start()
            else:
                @pl.when(c == x)
                def _():
                    pltpu.make_async_copy(src, lowr.at[pl.ds(mine, GR), :], rsem.at[base + x]).start()

                @pl.when(c != x)
                def _():
                    cp.start()

    x_b[1].wait_recv()
    k_xmb = on_chip(xo, zm, RA, RB)
    x_b[2].wait_recv()
    k_xpb = on_chip(xo, zp, RA, RB)
    emit(c, (xo, p))
    for cp in (k_xa, k_xb, k_xpa, k_xma, k_xmb, k_xpb):
        cp.wait_recv()
    emit(co, (xo, p))
    p_f1.wait_recv()
    k_oa = on_chip(x, zo, 0, RA)
    m_f1.wait_recv()
    k_xoa = on_chip(xo, zo, 0, RA)
    x_b[3].wait_recv()
    k_xob = on_chip(xo, zo, RA, RB)
    emit(c, (x, 1 - p))
    for cp in (k_ob, k_oa):
        cp.wait_recv()
    emit(co, (x, 1 - p))
    emit(c, (xo, 1 - p))
    for cp in (k_xoa, k_xob):
        cp.wait_recv()
    emit(co, (xo, 1 - p))
    avg_cp.wait()
    lanes = pl.ds(pl.multiple_of((z * NC + c) * LR, LR), LR)
    some = lowr.at[pl.ds(0, GR), :]
    for pp, shifts in ((p, (0, lax.rem(z - zf + NZ, NZ))), (1 - p, (2, lax.rem(z - zof + NZ, NZ)))):
        for xx in (x, xo):
            for dz in shifts:
                pltpu.make_async_copy(some, some, rsem.at[base + dz * NX + xx]).wait()
            first = pair_cols(xx, pp)

            @pl.loop(0, PR // 128)
            def _(j):
                cols = pl.ds(pl.multiple_of(first + j * 128, 128), 128)
                nw = wts[x, cols, lanes].astype(F32) + lowr[cols, :].astype(F32)
                o_avg[:, cols] = average_decay * avg_in[:, cols] + (1.0 - average_decay) * nw.T

    for cp in out_own:
        cp.wait()
    for cp in out_oth:
        cp.wait_recv()
    for cp in started:
        cp.wait_send()
    for i, cp in enumerate(low_cp):
        if i:
            cp.wait_send()
        else:
            @pl.when(c != x)
            def _():
                cp.wait_send()


def store(*refs):
    sems = refs[-1]
    n = (len(refs) - 1) // 2
    copies = []
    for src, dst in zip(refs[:n], refs[n:2 * n]):
        rows = src.shape[0]
        parts = 8 if rows > 1024 else 1
        for i in range(parts):
            r = pl.ds(i * (rows // parts), rows // parts)
            copies.append(pltpu.make_async_copy(src.at[r, :], dst.at[r, :], sems.at[len(copies)]))
    for cp in copies:
        cp.start()
    for cp in copies:
        cp.wait()


def local(dims, grads, gain_grads, master, moment1, moment2, average, gain_master, gain_m, gain_v):
    D, BW, NS, NT = dims
    H, CH = D // 2, BW // 16
    GR = 2 * CH
    RA = 112 * GR // 192
    RB = GR - RA
    LN = min(128, H)
    vm, sem = pltpu.VMEM, pltpu.SemaphoreType
    hbm = pl.BlockSpec(memory_space=pltpu.HBM)
    vmem = pl.BlockSpec(memory_space=pltpu.VMEM)
    shape = lambda sh, dt=F32: jax.ShapeDtypeStruct(sh, dt)
    outs = pl.pallas_call(
        functools.partial(kernel, dims),
        out_shape=(shape((CH, D)), shape((CH, D)), shape((CH, D)), shape((D, BW), BF16),
                   shape((D // 16, BW)), shape((1, D)), shape((1, D)), shape((1, D))),
        in_specs=[hbm] * 9,
        out_specs=[vmem] * 8,
        scratch_shapes=[
            vm((2, H, BW), BF16),
            vm((BW, H), F32),
            vm((2, 2, RA // 2, H), F32),
            vm((2, 4, RA // 2, H), F32),
            vm((RA, H), F32),
            vm((4, RB, H), F32),
            vm((2, RB // 2, H), F32),
            vm((4, RB // 2, H), F32),
            vm((3, GR, H), F32),
            vm((2, BW, H), BF16),
            vm((GR, H), BF16),
            vm((BW, D // 16), BF16),
            vm((D // 16, BW), F32),
            vm((4, 1, D), F32),
            vm((6, H, 128), BF16),
            vm((9, 8, LN), F32),
            vm((NX * NS * NT + 1, 8, LN), F32),
            vm((8, 1, D), F32),
            vm((NX * NT, 1, D), F32),
            sem.DMA((32,)),
            sem.DMA((120,)),
            sem.DMA((120,)),
            sem.DMA((8,)),
            vm((1, D), F32),
        ],
        compiler_params=pltpu.CompilerParams(
            collective_id=0, has_side_effects=True, vmem_limit_bytes=36 * 2**20),
        name="adamw_step",
    )(*[pltpu.with_memory_space_constraint(a, pltpu.HBM) for a in (
        grads[0, 0, 0], gain_grads[0], master[0, 0], moment1[0, 0], moment2[0, 0], average[0, 0],
        gain_master, gain_m, gain_v)])
    outs = pl.pallas_call(
        store,
        out_shape=[shape(o.shape, o.dtype) for o in outs],
        in_specs=[pl.BlockSpec(memory_space=pl.ANY)] * 8,
        out_specs=[pl.BlockSpec(memory_space=pl.ANY)] * 8,
        scratch_shapes=[sem.DMA((32,))],
        compiler_params=pltpu.CompilerParams(vmem_limit_bytes=2**20),
        name="store",
    )(*outs)
    new_master, new_m, new_v, weights, new_average, g, gm, gv = outs
    return (new_master[None, None], new_m[None, None], new_v[None, None], weights[None, None],
            new_average[None, None], g, gm, gv)


def solution(mesh):
    whole = P("section", "tensor", "shard", None)
    gains = P("section", None)

    def step(grads, *rest):
        dims = (grads.shape[3], grads.shape[4], mesh.shape["section"], mesh.shape["tensor"])
        return jax.shard_map(
            functools.partial(local, dims),
            mesh=mesh,
            in_specs=(P("section", "tensor", "shard", None, None), P("section", ("shard", "tensor"), None),
                      whole, whole, whole, whole, gains, gains, gains),
            out_specs=(whole, whole, whole, P("section", "tensor", None, None), whole, gains, gains, gains),
            check_vma=False,
        )(grads, *rest)

    return step
```
